512 devices in a mesh: blk: 16 (over z, y_hi), tm: 32 (over y_lo, x, core).
Axes of the slice: x: 4, y: 8 (y_hi: 2, y_lo: 4; y = y_hi * 4 + y_lo), z: 8, core: 2. Of those that a mesh axis runs over, the one named last changes fastest.
Arguments:
- spectra: bfloat16 [2, 512, 256, 2048], P(None, None, 'tm', 'blk'), may hold values from -6 to 6
- picks: int32 [4, 32], P(None, 'blk'), may hold values from 0 to 127
Outputs:
- correlations: float32 [4, 512, 2, 2048], P(None, 'tm', None, 'blk')
The draws below stay inside these ranges and needn't reach their ends.
All inputs are finite; a program needn't handle non-finite values.
Results may differ from the reference program's by a relative error of at most 0.0003.
Values may be sent and summed in bfloat16 or wider, within the bound.
A program may use at most 64 MiB of HBM per device.

```python
import math
import jax
import jax.numpy as jnp
from jax import lax

F = 512
LAGS = 512
C_DEV = 128
SRC = 2
STEPS = 4
WINDOWS = 256
CHANNELS = 2048
SOURCES = 32
N_BLK = 16


def touch_ends(array, own_key, low, top_value):
    longest = array.shape.index(max(array.shape))
    spots = []
    for shift in (0, 1):
        where = [jax.random.randint(jax.random.fold_in(own_key, axis), (), 0, length) for axis, length in enumerate(array.shape)]
        where[longest] = (where[longest] + shift) % array.shape[longest]
        spots.append(tuple(where))
    return array.at[spots[0]].set(low).at[spots[1]].set(top_value)


def levels(own_key, dims, pieces, smallest, high):
    level = 1.0
    for axis_at, blocks in pieces:
        heights = jax.random.uniform(jax.random.fold_in(jax.random.fold_in(own_key, 6), axis_at), (blocks,), jnp.float32, smallest / len(pieces), high / len(pieces))
        level = level * jnp.repeat(jnp.exp(heights), dims[axis_at] // blocks).reshape((-1,) + (1,) * (len(dims) - 1 - axis_at))
    return level


def noise(rng, shape, spread, limit, cuts=(), kind=jnp.bfloat16):
    level = levels(rng, shape, cuts, -0.22, 0.18) if cuts else 1.0
    drawn = jax.random.normal(rng, shape, jnp.float32) * spread * level
    return jnp.minimum(jnp.maximum(drawn, -limit), limit).astype(kind)


def setup_inputs(seed: int = 0) -> dict:
    key_of = jax.random.split(jax.random.key(seed), 3)
    return {
        "spectra": noise(key_of[0], (2, F, WINDOWS, CHANNELS), 1.0, 6.0, ((2, 32), (3, 16))),
        "picks": touch_ends(jax.random.randint(key_of[1], (STEPS, SOURCES), 0, C_DEV), jax.random.fold_in(key_of[1], 1), 0, C_DEV - 1).astype(jnp.int32),
    }


def lag_table(start, count, freqs, lags, scale_factor):
    lag_rows = start + jnp.arange(count, dtype=jnp.int32)
    freq_cols = jnp.arange(freqs, dtype=jnp.int32)
    phase = lag_rows[:, None] * freq_cols[None, :] % lags
    angle = 2.0 * math.pi / lags * phase.astype(jnp.float32)
    return jnp.concatenate([jnp.cos(angle), -jnp.sin(angle)], axis=1) * scale_factor

def cross_exact(source, receive):
    high = lax.Precision.HIGHEST
    part_re = jnp.einsum('fws,fwc->fsc', source[0], receive[0], precision=high) + jnp.einsum('fws,fwc->fsc', source[1], receive[1], precision=high)
    part_im = jnp.einsum('fws,fwc->fsc', source[0], receive[1], precision=high) - jnp.einsum('fws,fwc->fsc', source[1], receive[0], precision=high)
    freqs = part_re.shape[0]
    return jnp.concatenate([part_re.reshape(freqs, -1), part_im.reshape(freqs, -1)], axis=0)

def reference(spectra, picks):
    scale_factor = 1.0 / math.sqrt(F * WINDOWS)
    table = lag_table(0, LAGS, F, LAGS, scale_factor)
    results = []
    for turn_index in range(STEPS):

        def one_block(block):
            anchor = (block - turn_index) % N_BLK
            chosen = lax.dynamic_slice_in_dim(picks[turn_index], (anchor * SRC).astype(jnp.int32), SRC) + (anchor * C_DEV).astype(jnp.int32)
            source = jnp.take(spectra, chosen, axis=3).astype(jnp.float32)
            receive = lax.dynamic_slice_in_dim(spectra, (block * C_DEV).astype(jnp.int32), C_DEV, 3).astype(jnp.float32)
            stacked = cross_exact(source, receive)
            lagged = jnp.dot(table, stacked, precision=lax.Precision.HIGHEST, preferred_element_type=jnp.float32)
            return lagged.reshape(LAGS, SRC, C_DEV)
        blocks = lax.map(one_block, jnp.arange(N_BLK, dtype=jnp.int32))
        results.append(jnp.transpose(blocks, (1, 2, 0, 3)).reshape(LAGS, SRC, CHANNELS))
    return jnp.stack(results)
```

```python
import functools
import math

import jax
import jax.numpy as jnp
import ml_dtypes
import numpy as np
from jax import lax
from jax.experimental import pallas as pl
from jax.experimental.pallas import tpu as pltpu
from jax.sharding import PartitionSpec as P

F = 512
LAGS = 512
W = 8
C = 128
STEPS = 4
SRC = 2
G = 32
NG = F // G
NX = 4
NY = 4
ROWS = 16
COLS = SRC * C
MESH = pl.DeviceIdType.MESH


def tables(windows):
    scale = 1.0 / math.sqrt(F * windows)
    core, x, ylo, i = np.meshgrid(np.arange(2), np.arange(NX), np.arange(2), np.arange(ROWS), indexing="ij")
    lag = (ylo * 128 + x * 32 + core * 16 + i).reshape(2, 1, 128, 1)
    freq = 2 * np.arange(F // 2)[None, :] + np.arange(2)[:, None]
    angle = 2.0 * np.pi / LAGS * (lag * freq.reshape(1, 2, 1, F // 2) % LAGS)
    full = (np.concatenate([np.cos(angle), -np.sin(angle)], axis=3) * scale).astype(np.float32)
    high = full.astype(ml_dtypes.bfloat16)
    low = (full - high.astype(np.float32)).astype(ml_dtypes.bfloat16)
    return np.stack([high, low], axis=1)


def kernel(
    spec_hbm, table_hbm, picks, out,
    spec, table, rows, src_out, src_in, x_ref, part, core_in, x_in, summed, y_in,
    load_sem, src_s, src_r, core_s, core_r, x_s, x_r, y_s, y_r,
):
    blk = lax.axis_index("blk")
    tm = lax.axis_index("tm")
    core = tm % 2
    xpos = (tm // 2) % NX
    ypos = tm // (2 * NX)
    n_blk = lax.axis_size("blk")

    def at(y, x, c):
        return {"tm": (y * NX + x) * 2 + c}

    load_spec = pltpu.make_async_copy(spec_hbm, spec, load_sem.at[0])
    load_table = pltpu.make_async_copy(table_hbm, table, load_sem.at[1])
    load_spec.start()
    load_table.start()

    barrier = pltpu.get_barrier_semaphore()
    peers = [at(ypos, xpos, 1 - core)]
    peers += [at(ypos, (xpos + d) % NX, core) for d in range(1, NX)]
    peers += [at((ypos + d) % NY, xpos, core) for d in range(1, NY)]
    for k in range(1, STEPS):
        peers += [{"blk": (blk + k) % n_blk}, {"blk": (blk + n_blk - k) % n_blk}]
    for peer in peers:
        pl.semaphore_signal(barrier, inc=1, device_id=peer, device_id_type=MESH)

    row_id = lax.broadcasted_iota(jnp.int32, (16, C), 0)
    lane_id = lax.broadcasted_iota(jnp.int32, (16, C), 1)
    chosen = jnp.full((16, C), -1, jnp.int32)
    for k in range(STEPS):
        for s in range(SRC):
            chosen = jnp.where(row_id == k * SRC + s, picks[k, s], chosen)
    one_hot = jnp.where(lane_id == chosen, 1.0, 0.0).astype(jnp.bfloat16)

    load_spec.wait()

    def select(g, carry):
        for p in range(2):
            got = lax.dot_general(
                one_hot, spec[p, pl.ds(pl.multiple_of(g * G * W, G * W), G * W), :],
                (((1,), (1,)), ((), ())), preferred_element_type=jnp.float32,
            )
            for k in range(STEPS):
                for s in range(SRC):
                    r = k * SRC + s
                    rows[k, pl.ds((p * SRC + s) * NG + g, 1), :] = got[r : r + 1, :]
        return carry

    lax.fori_loop(0, NG, select, 0)
    for k in range(1, STEPS):
        src_out[k - 1] = rows[k].astype(jnp.bfloat16)
    pl.semaphore_wait(barrier, len(peers))

    src_copies = []
    for k in (2, 1, 3):
        copy = pltpu.make_async_remote_copy(
            src_ref=src_out.at[k - 1], dst_ref=src_in.at[k - 1],
            send_sem=src_s.at[k - 1], recv_sem=src_r.at[k - 1],
            device_id={"blk": (blk + k) % n_blk}, device_id_type=MESH,
        )
        copy.start()
        src_copies.append(copy)

    r_id = lax.broadcasted_iota(jnp.int32, (G, G * W), 0)
    l_id = lax.broadcasted_iota(jnp.int32, (G, G * W), 1)
    half = G // 2
    wanted = jnp.where(r_id < half, 2 * r_id, 2 * (r_id - half) + 1)
    mask = jnp.where(l_id // W == wanted, 1.0, 0.0)

    def cross(steps):
        def body(g, carry):
            block = pl.ds(pl.multiple_of(g * G * W, G * W), G * W)
            b_re = spec[0, block, :]
            b_im = spec[1, block, :]
            total = None
            for p in range(2):
                left = [
                    (rows[k, pl.ds((p * SRC + s) * NG + g, 1), :] * mask).astype(jnp.bfloat16)
                    for k in steps
                    for s in range(SRC)
                ]
                right = [b_re, b_im] if p == 0 else [b_im, -b_re]
                term = jnp.dot(
                    jnp.concatenate(left, axis=0), jnp.concatenate(right, axis=1),
                    preferred_element_type=jnp.float32,
                )
                total = term if total is None else total + term
            high = total.astype(jnp.bfloat16)
            low = (total - high.astype(jnp.float32)).astype(jnp.bfloat16)
            for hl, value in enumerate((high, low)):
                for j, k in enumerate(steps):
                    for s in range(SRC):
                        for eo in range(2):
                            top = (j * SRC + s) * G + eo * half
                            for ri in range(2):
                                x_ref[
                                    k, hl, eo,
                                    pl.ds(pl.multiple_of(ri * (F // 2) + g * half, half), half),
                                    s * C : (s + 1) * C,
                                ] = value[top : top + half, ri * C : (ri + 1) * C]
            return carry

        lax.fori_loop(0, NG, body, 0)

    def transform(k):
        for h in range(2):
            both = []
            for eo in range(2):
                high = x_ref[k, 0, eo]
                low = x_ref[k, 1, eo]
                both.append(
                    jnp.dot(table[h, 0, eo], high, preferred_element_type=jnp.float32)
                    + jnp.dot(table[h, 0, eo], low, preferred_element_type=jnp.float32)
                    + jnp.dot(table[h, 1, eo], high, preferred_element_type=jnp.float32)
                )
            plus = both[0] + both[1]
            minus = both[0] - both[1]
            for x in range(NX):
                part[k, h, x, 0:32, :] = plus[x * 32 : x * 32 + 32]
                part[k, h, x, 32:64, :] = minus[x * 32 : x * 32 + 32]

    core_copies, x_copies, y_copies = {}, {}, {}

    def send_core(k):
        copy = pltpu.make_async_remote_copy(
            src_ref=part.at[k, 1 - core], dst_ref=core_in.at[k],
            send_sem=core_s.at[k], recv_sem=core_r.at[k],
            device_id=at(ypos, xpos, 1 - core), device_id_type=MESH,
        )
        copy.start()
        core_copies[k] = copy

    def send_x(k):
        core_copies[k].wait_recv()
        part[k, core] = part[k, core] + core_in[k]
        for d in (2, 1, 3):
            copy = pltpu.make_async_remote_copy(
                src_ref=part.at[k, core, (xpos + d) % NX], dst_ref=x_in.at[k, d - 1],
                send_sem=x_s.at[k, d - 1], recv_sem=x_r.at[k, d - 1],
                device_id=at(ypos, (xpos + d) % NX, core), device_id_type=MESH,
            )
            copy.start()
            x_copies[k, d] = copy

    def send_y(k):
        for d in range(1, NX):
            x_copies[k, d].wait_recv()
        total = part[k, core, xpos] + x_in[k, 0] + x_in[k, 1] + x_in[k, 2]
        for y in range(NY):
            summed[k, y] = total[y * ROWS : (y + 1) * ROWS]
        for d in range(1, NY):
            copy = pltpu.make_async_remote_copy(
                src_ref=summed.at[k, (ypos + d) % NY], dst_ref=y_in.at[k, d - 1],
                send_sem=y_s.at[k, d - 1], recv_sem=y_r.at[k, d - 1],
                device_id=at((ypos + d) % NY, xpos, core), device_id_type=MESH,
            )
            copy.start()
            y_copies[k, d] = copy

    def finish(k):
        for d in range(1, NY):
            y_copies[k, d].wait_recv()
        total = summed[k, ypos] + y_in[k, 0] + y_in[k, 1] + y_in[k, 2]
        for s in range(SRC):
            out[k, s] = total[:, s * C : (s + 1) * C]

    cross((0,))
    load_table.wait()
    transform(0)
    send_core(0)
    for copy in src_copies:
        copy.wait_recv()
    for k in range(1, STEPS):
        rows[k] = src_in[k - 1].astype(jnp.float32)
    send_x(0)
    cross((1, 2, 3))
    for k in range(1, STEPS):
        transform(k)
        send_core(k)
        if k > 1:
            send_x(k - 1)
    send_y(0)
    send_x(STEPS - 1)
    for k in range(1, STEPS):
        send_y(k)
        finish(k - 1)
    finish(STEPS - 1)
    for copy in [*src_copies, *core_copies.values(), *x_copies.values(), *y_copies.values()]:
        copy.wait_send()


def local(spectra, picks):
    freqs, width, chans = spectra.shape[1:]
    table = jnp.asarray(tables(width * lax.axis_size("tm")))
    dma = pltpu.SemaphoreType.DMA
    scratch = [
        pltpu.VMEM((2, F * W, C), jnp.bfloat16),
        pltpu.VMEM(table.shape, jnp.bfloat16),
        pltpu.VMEM((STEPS, 2 * SRC * NG, G * W), jnp.float32),
        pltpu.VMEM((STEPS - 1, 2 * SRC * NG, G * W), jnp.bfloat16),
        pltpu.VMEM((STEPS - 1, 2 * SRC * NG, G * W), jnp.bfloat16),
        pltpu.VMEM((STEPS, 2, 2, F, COLS), jnp.bfloat16),
        pltpu.VMEM((STEPS, 2, NX, NY * ROWS, COLS), jnp.float32),
        pltpu.VMEM((STEPS, NX, NY * ROWS, COLS), jnp.float32),
        pltpu.VMEM((STEPS, NX - 1, NY * ROWS, COLS), jnp.float32),
        pltpu.VMEM((STEPS, NY, ROWS, COLS), jnp.float32),
        pltpu.VMEM((STEPS, NY - 1, ROWS, COLS), jnp.float32),
        dma((2,)), dma((STEPS - 1,)), dma((STEPS - 1,)), dma((STEPS,)), dma((STEPS,)),
        dma((STEPS, NX - 1)), dma((STEPS, NX - 1)), dma((STEPS, NY - 1)), dma((STEPS, NY - 1)),
    ]
    any_space = pl.BlockSpec(memory_space=pl.ANY)
    got = pl.pallas_call(
        kernel,
        out_shape=jax.ShapeDtypeStruct((STEPS, SRC, ROWS, C), jnp.float32),
        in_specs=[any_space, any_space, pl.BlockSpec(memory_space=pltpu.SMEM)],
        out_specs=pl.BlockSpec(memory_space=pltpu.VMEM),
        scratch_shapes=scratch,
        compiler_params=pltpu.CompilerParams(
            collective_id=0, has_side_effects=True, vmem_limit_bytes=40 * 1024 * 1024
        ),
        name="correlate",
    )(spectra.reshape(2, freqs * width, chans), table, picks)
    return jnp.transpose(got, (0, 2, 1, 3))


def solution(mesh):
    placed = (P(None, None, "tm", "blk"), P(None, "blk"))
    return jax.shard_map(
        local, mesh=mesh, in_specs=placed, out_specs=P(None, "tm", None, "blk"), check_vma=False
    )
```

```python
import functools
import math

import jax
import jax.numpy as jnp
import ml_dtypes
import numpy as np
from jax import lax
from jax.experimental import pallas as pl
from jax.experimental.pallas import tpu as pltpu
from jax.sharding import PartitionSpec as P

F = 512
LAGS = 512
W = 8
C = 128
STEPS = 4
SRC = 2
G = 32
NG = F // G
NX = 4
NY = 4
ROWS = 16
COLS = SRC * C
MESH = pl.DeviceIdType.MESH


def tables(windows):
    scale = 1.0 / math.sqrt(F * windows)
    core, x, ylo, i = np.meshgrid(np.arange(2), np.arange(NX), np.arange(2), np.arange(ROWS), indexing="ij")
    lag = (ylo * 128 + x * 32 + core * 16 + i).reshape(2, 1, 128, 1)
    freq = 2 * np.arange(F // 2)[None, :] + np.arange(2)[:, None]
    angle = 2.0 * np.pi / LAGS * (lag * freq.reshape(1, 2, 1, F // 2) % LAGS)
    full = (np.concatenate([np.cos(angle), -np.sin(angle)], axis=3) * scale).astype(np.float32)
    high = full.astype(ml_dtypes.bfloat16)
    low = (full - high.astype(np.float32)).astype(ml_dtypes.bfloat16)
    return np.stack([high, low], axis=1)


def kernel(
    spec_hbm, table_hbm, picks, out,
    spec, table, rows, src_out, src_in, x_ref, part, core_in, x_in, summed, y_in,
    load_sem, src_s, src_r, core_s, core_r, x_s, x_r, y_s, y_r,
):
    blk = lax.axis_index("blk")
    tm = lax.axis_index("tm")
    core = tm % 2
    xpos = (tm // 2) % NX
    ypos = tm // (2 * NX)
    n_blk = lax.axis_size("blk")

    def at(y, x, c):
        return {"tm": (y * NX + x) * 2 + c}

    load_spec = pltpu.make_async_copy(spec_hbm, spec, load_sem.at[0])
    load_table = pltpu.make_async_copy(table_hbm, table, load_sem.at[1])
    load_spec.start()
    load_table.start()

    barrier = pltpu.get_barrier_semaphore()
    peers = [at(ypos, xpos, 1 - core)]
    peers += [at(ypos, (xpos + d) % NX, core) for d in range(1, NX)]
    peers += [at((ypos + d) % NY, xpos, core) for d in range(1, NY)]
    for k in range(1, STEPS):
        peers += [{"blk": (blk + k) % n_blk}, {"blk": (blk + n_blk - k) % n_blk}]
    for peer in peers:
        pl.semaphore_signal(barrier, inc=1, device_id=peer, device_id_type=MESH)

    row_id = lax.broadcasted_iota(jnp.int32, (16, C), 0)
    lane_id = lax.broadcasted_iota(jnp.int32, (16, C), 1)
    chosen = jnp.full((16, C), -1, jnp.int32)
    for k in range(STEPS):
        for s in range(SRC):
            chosen = jnp.where(row_id == k * SRC + s, picks[s, k], chosen)
    one_hot = jnp.where(lane_id == chosen, 1.0, 0.0).astype(jnp.bfloat16)

    load_spec.wait()

    def select(g, carry):
        for p in range(2):
            got = lax.dot_general(
                one_hot, spec[p, pl.ds(pl.multiple_of(g * G * W, G * W), G * W), :],
                (((1,), (1,)), ((), ())), preferred_element_type=jnp.float32,
            )
            for k in range(STEPS):
                for s in range(SRC):
                    r = k * SRC + s
                    rows[k, pl.ds((p * SRC + s) * NG + g, 1), :] = got[r : r + 1, :]
        return carry

    lax.fori_loop(0, NG, select, 0, unroll=4)
    for k in range(1, STEPS):
        src_out[k - 1] = rows[k].astype(jnp.bfloat16)
    pl.semaphore_wait(barrier, len(peers))

    src_copies = {}
    for k in (2, 1, 3):
        copy = pltpu.make_async_remote_copy(
            src_ref=src_out.at[k - 1], dst_ref=src_in.at[k - 1],
            send_sem=src_s.at[k - 1], recv_sem=src_r.at[k - 1],
            device_id={"blk": (blk + k) % n_blk}, device_id_type=MESH,
        )
        copy.start()
        src_copies[k] = copy

    r_id = lax.broadcasted_iota(jnp.int32, (G, G * W), 0)
    l_id = lax.broadcasted_iota(jnp.int32, (G, G * W), 1)
    half = G // 2
    wanted = jnp.where(r_id < half, 2 * r_id, 2 * (r_id - half) + 1)
    mask = jnp.where(l_id // W == wanted, 1.0, 0.0)

    def cross(steps):
        def body(g, carry):
            block = pl.ds(pl.multiple_of(g * G * W, G * W), G * W)
            b_re = spec[0, block, :]
            b_im = spec[1, block, :]
            total = None
            for p in range(2):
                left = [
                    (rows[k, pl.ds((p * SRC + s) * NG + g, 1), :] * mask).astype(jnp.bfloat16)
                    for k in steps
                    for s in range(SRC)
                ]
                right = [b_re, b_im] if p == 0 else [b_im, -b_re]
                term = jnp.dot(
                    jnp.concatenate(left, axis=0), jnp.concatenate(right, axis=1),
                    preferred_element_type=jnp.float32,
                )
                total = term if total is None else total + term
            high = total.astype(jnp.bfloat16)
            low = (total - high.astype(jnp.float32)).astype(jnp.bfloat16)
            for hl, value in enumerate((high, low)):
                for j, k in enumerate(steps):
                    for s in range(SRC):
                        for eo in range(2):
                            top = (j * SRC + s) * G + eo * half
                            for ri in range(2):
                                x_ref[
                                    k, hl, eo,
                                    pl.ds(pl.multiple_of(ri * (F // 2) + g * half, half), half),
                                    s * C : (s + 1) * C,
                                ] = value[top : top + half, ri * C : (ri + 1) * C]
            return carry

        lax.fori_loop(0, NG, body, 0, unroll=4)

    def transform(k):
        for h in range(2):
            both = []
            for eo in range(2):
                high = x_ref[k, 0, eo]
                low = x_ref[k, 1, eo]
                both.append(
                    jnp.dot(table[h, 0, eo], high, preferred_element_type=jnp.float32)
                    + jnp.dot(table[h, 0, eo], low, preferred_element_type=jnp.float32)
                    + jnp.dot(table[h, 1, eo], high, preferred_element_type=jnp.float32)
                )
            plus = both[0] + both[1]
            minus = both[0] - both[1]
            for x in range(NX):
                part[k, h, x, 0:32, :] = plus[x * 32 : x * 32 + 32]
                part[k, h, x, 32:64, :] = minus[x * 32 : x * 32 + 32]

    core_copies, x_copies, y_copies = {}, {}, {}

    def send_core(k):
        copy = pltpu.make_async_remote_copy(
            src_ref=part.at[k, 1 - core], dst_ref=core_in.at[k],
            send_sem=core_s.at[k], recv_sem=core_r.at[k],
            device_id=at(ypos, xpos, 1 - core), device_id_type=MESH,
        )
        copy.start()
        core_copies[k] = copy

    def send_x(k):
        core_copies[k].wait_recv()
        part[k, core] = part[k, core] + core_in[k]
        for d in (2, 1, 3):
            copy = pltpu.make_async_remote_copy(
                src_ref=part.at[k, core, (xpos + d) % NX], dst_ref=x_in.at[k, d - 1],
                send_sem=x_s.at[k, d - 1], recv_sem=x_r.at[k, d - 1],
                device_id=at(ypos, (xpos + d) % NX, core), device_id_type=MESH,
            )
            copy.start()
            x_copies[k, d] = copy

    def send_y(k):
        for d in range(1, NX):
            x_copies[k, d].wait_recv()
        total = part[k, core, xpos] + x_in[k, 0] + x_in[k, 1] + x_in[k, 2]
        for y in range(NY):
            summed[k, y] = total[y * ROWS : (y + 1) * ROWS]
        for d in range(1, NY):
            copy = pltpu.make_async_remote_copy(
                src_ref=summed.at[k, (ypos + d) % NY], dst_ref=y_in.at[k, d - 1],
                send_sem=y_s.at[k, d - 1], recv_sem=y_r.at[k, d - 1],
                device_id=at((ypos + d) % NY, xpos, core), device_id_type=MESH,
            )
            copy.start()
            y_copies[k, d] = copy

    def finish(k):
        for d in range(1, NY):
            y_copies[k, d].wait_recv()
        total = summed[k, ypos] + y_in[k, 0] + y_in[k, 1] + y_in[k, 2]
        for s in range(SRC):
            out[k, s] = total[:, s * C : (s + 1) * C]

    def step(k):
        if k > 0:
            src_copies[k].wait_recv()
            rows[k] = src_in[k - 1].astype(jnp.float32)
        cross((k,))
        if k == 0:
            load_table.wait()
        transform(k)
        send_core(k)

    step(0)
    step(2)
    send_x(0)
    send_x(2)
    step(1)
    send_y(0)
    step(3)
    send_x(1)
    send_y(2)
    send_x(3)
    finish(0)
    finish(2)
    send_y(1)
    send_y(3)
    finish(1)
    finish(3)
    for copy in [*src_copies.values(), *core_copies.values(), *x_copies.values(), *y_copies.values()]:
        copy.wait_send()


def local(spectra, picks):
    freqs, width, chans = spectra.shape[1:]
    table = jnp.asarray(tables(width * lax.axis_size("tm")))
    dma = pltpu.SemaphoreType.DMA
    scratch = [
        pltpu.VMEM((2, F * W, C), jnp.bfloat16),
        pltpu.VMEM(table.shape, jnp.bfloat16),
        pltpu.VMEM((STEPS, 2 * SRC * NG, G * W), jnp.float32),
        pltpu.VMEM((STEPS - 1, 2 * SRC * NG, G * W), jnp.bfloat16),
        pltpu.VMEM((STEPS - 1, 2 * SRC * NG, G * W), jnp.bfloat16),
        pltpu.VMEM((STEPS, 2, 2, F, COLS), jnp.bfloat16),
        pltpu.VMEM((STEPS, 2, NX, NY * ROWS, COLS), jnp.float32),
        pltpu.VMEM((STEPS, NX, NY * ROWS, COLS), jnp.float32),
        pltpu.VMEM((STEPS, NX - 1, NY * ROWS, COLS), jnp.float32),
        pltpu.VMEM((STEPS, NY, ROWS, COLS), jnp.float32),
        pltpu.VMEM((STEPS, NY - 1, ROWS, COLS), jnp.float32),
        dma((2,)), dma((STEPS - 1,)), dma((STEPS - 1,)), dma((STEPS,)), dma((STEPS,)),
        dma((STEPS, NX - 1)), dma((STEPS, NX - 1)), dma((STEPS, NY - 1)), dma((STEPS, NY - 1)),
    ]
    any_space = pl.BlockSpec(memory_space=pl.ANY)
    got = pl.pallas_call(
        kernel,
        out_shape=jax.ShapeDtypeStruct((STEPS, SRC, ROWS, C), jnp.float32),
        in_specs=[any_space, any_space, pl.BlockSpec(memory_space=pltpu.SMEM)],
        out_specs=pl.BlockSpec(memory_space=pltpu.VMEM),
        scratch_shapes=scratch,
        compiler_params=pltpu.CompilerParams(
            collective_id=0, has_side_effects=True, vmem_limit_bytes=62 * 1024 * 1024
        ),
        name="correlate",
    )(spectra.reshape(2, freqs * width, chans), table, picks.T)
    return jnp.transpose(got, (0, 2, 1, 3))


def solution(mesh):
    placed = (P(None, None, "tm", "blk"), P(None, "blk"))
    return jax.shard_map(
        local, mesh=mesh, in_specs=placed, out_specs=P(None, "tm", None, "blk"), check_vma=False
    )
```

```python
import functools
import math

import jax
import jax.numpy as jnp
import ml_dtypes
import numpy as np
from jax import lax
from jax.experimental import pallas as pl
from jax.experimental.pallas import tpu as pltpu
from jax.sharding import PartitionSpec as P

F = 512
LAGS = 512
W = 8
C = 128
STEPS = 4
SRC = 2
G = 32
NG = F // G
NX = 4
NY = 4
ROWS = 16
COLS = SRC * C
MESH = pl.DeviceIdType.MESH


def tables(windows):
    scale = 1.0 / math.sqrt(F * windows)
    core, x, ylo, i = np.meshgrid(np.arange(2), np.arange(NX), np.arange(2), np.arange(ROWS), indexing="ij")
    lag = (ylo * 128 + x * 32 + core * 16 + i).reshape(2, 1, 128, 1)
    freq = 2 * np.arange(F // 2)[None, :] + np.arange(2)[:, None]
    angle = 2.0 * np.pi / LAGS * (lag * freq.reshape(1, 2, 1, F // 2) % LAGS)
    full = (np.concatenate([np.cos(angle), -np.sin(angle)], axis=3) * scale).astype(np.float32)
    high = full.astype(ml_dtypes.bfloat16)
    low = (full - high.astype(np.float32)).astype(ml_dtypes.bfloat16)
    return np.stack([high, low], axis=1)


def kernel(
    spec_hbm, table_hbm, picks, out,
    spec, table, rows, src_out, src_in, x_ref, part, core_in, x_in, summed, y_in,
    load_sem, src_s, src_r, core_s, core_r, x_s, x_r, y_s, y_r,
):
    blk = lax.axis_index("blk")
    tm = lax.axis_index("tm")
    core = tm % 2
    xpos = (tm // 2) % NX
    ypos = tm // (2 * NX)
    n_blk = lax.axis_size("blk")

    def at(y, x, c):
        return {"tm": (y * NX + x) * 2 + c}

    load_spec = pltpu.make_async_copy(spec_hbm, spec, load_sem.at[0])
    load_table = pltpu.make_async_copy(table_hbm, table, load_sem.at[1])
    load_spec.start()
    load_table.start()

    barrier = pltpu.get_barrier_semaphore()
    peers = [at(ypos, xpos, 1 - core)]
    peers += [at(ypos, (xpos + d) % NX, core) for d in range(1, NX)]
    peers += [at((ypos + d) % NY, xpos, core) for d in range(1, NY)]
    for k in range(1, STEPS):
        peers += [{"blk": (blk + k) % n_blk}, {"blk": (blk + n_blk - k) % n_blk}]
    for peer in peers:
        pl.semaphore_signal(barrier, inc=1, device_id=peer, device_id_type=MESH)

    row_id = lax.broadcasted_iota(jnp.int32, (16, C), 0)
    lane_id = lax.broadcasted_iota(jnp.int32, (16, C), 1)
    chosen = jnp.full((16, C), -1, jnp.int32)
    for k in range(STEPS):
        for s in range(SRC):
            chosen = jnp.where(row_id == k * SRC + s, picks[s, k], chosen)
    one_hot = jnp.where(lane_id == chosen, 1.0, 0.0).astype(jnp.bfloat16)

    load_spec.wait()

    def select(g, carry):
        for p in range(2):
            got = lax.dot_general(
                one_hot, spec[p, pl.ds(pl.multiple_of(g * G * W, G * W), G * W), :],
                (((1,), (1,)), ((), ())), preferred_element_type=jnp.float32,
            )
            for k in range(STEPS):
                for s in range(SRC):
                    r = k * SRC + s
                    rows[k, pl.ds((p * SRC + s) * NG + g, 1), :] = got[r : r + 1, :]
        return carry

    lax.fori_loop(0, NG, select, 0, unroll=8)
    for k in range(1, STEPS):
        src_out[k - 1] = rows[k].astype(jnp.bfloat16)
    r_id = lax.broadcasted_iota(jnp.int32, (G, G * W), 0)
    l_id = lax.broadcasted_iota(jnp.int32, (G, G * W), 1)
    half = G // 2
    wanted = jnp.where(r_id < half, 2 * r_id, 2 * (r_id - half) + 1)
    mask = jnp.where(l_id // W == wanted, 1.0, 0.0)

    def cross(k):
        def body(g, carry):
            block = pl.ds(pl.multiple_of(g * G * W, G * W), G * W)
            both = jnp.concatenate([spec[0, block, :], spec[1, block, :]], axis=1)
            left = [
                (rows[k, pl.ds((p * SRC + s) * NG + g, 1), :] * mask).astype(jnp.bfloat16)
                for p in range(2)
                for s in range(SRC)
            ]
            term = jnp.dot(jnp.concatenate(left, axis=0), both, preferred_element_type=jnp.float32)
            count = SRC * G
            parts = (
                term[:count, :C] + term[count:, C:],
                term[:count, C:] - term[count:, :C],
            )
            for ri, total in enumerate(parts):
                high = total.astype(jnp.bfloat16)
                low = (total - high.astype(jnp.float32)).astype(jnp.bfloat16)
                for hl, value in enumerate((high, low)):
                    for s in range(SRC):
                        for eo in range(2):
                            top = s * G + eo * half
                            x_ref[
                                k, hl, eo,
                                pl.ds(pl.multiple_of(ri * (F // 2) + g * half, half), half),
                                s * C : (s + 1) * C,
                            ] = value[top : top + half]
            return carry

        lax.fori_loop(0, NG, body, 0, unroll=8)

    def transform(k):
        for h in range(2):
            both = []
            for eo in range(2):
                high = x_ref[k, 0, eo]
                low = x_ref[k, 1, eo]
                both.append(
                    jnp.dot(table[h, 0, eo], high, preferred_element_type=jnp.float32)
                    + jnp.dot(table[h, 0, eo], low, preferred_element_type=jnp.float32)
                    + jnp.dot(table[h, 1, eo], high, preferred_element_type=jnp.float32)
                )
            plus = both[0] + both[1]
            minus = both[0] - both[1]
            for x in range(NX):
                part[k, h, x, 0:32, :] = plus[x * 32 : x * 32 + 32]
                part[k, h, x, 32:64, :] = minus[x * 32 : x * 32 + 32]

    core_copies, x_copies, y_copies = {}, {}, {}

    def send_core(k):
        copy = pltpu.make_async_remote_copy(
            src_ref=part.at[k, 1 - core], dst_ref=core_in.at[k],
            send_sem=core_s.at[k], recv_sem=core_r.at[k],
            device_id=at(ypos, xpos, 1 - core), device_id_type=MESH,
        )
        copy.start()
        core_copies[k] = copy

    def send_x(k):
        core_copies[k].wait_recv()
        part[k, core] = part[k, core] + core_in[k]
        for d in (2, 1, 3):
            copy = pltpu.make_async_remote_copy(
                src_ref=part.at[k, core, (xpos + d) % NX], dst_ref=x_in.at[k, d - 1],
                send_sem=x_s.at[k, d - 1], recv_sem=x_r.at[k, d - 1],
                device_id=at(ypos, (xpos + d) % NX, core), device_id_type=MESH,
            )
            copy.start()
            x_copies[k, d] = copy

    def send_y(k):
        for d in range(1, NX):
            x_copies[k, d].wait_recv()
        total = part[k, core, xpos] + x_in[k, 0] + x_in[k, 1] + x_in[k, 2]
        for y in range(NY):
            summed[k, y] = total[y * ROWS : (y + 1) * ROWS]
        for d in range(1, NY):
            copy = pltpu.make_async_remote_copy(
                src_ref=summed.at[k, (ypos + d) % NY], dst_ref=y_in.at[k, d - 1],
                send_sem=y_s.at[k, d - 1], recv_sem=y_r.at[k, d - 1],
                device_id=at((ypos + d) % NY, xpos, core), device_id_type=MESH,
            )
            copy.start()
            y_copies[k, d] = copy

    def finish(k):
        for d in range(1, NY):
            y_copies[k, d].wait_recv()
        total = summed[k, ypos] + y_in[k, 0] + y_in[k, 1] + y_in[k, 2]
        for s in range(SRC):
            out[k, s] = total[:, s * C : (s + 1) * C]

    def arrive(k):
        src_copies[k].wait_recv()
        rows[k] = src_in[k - 1].astype(jnp.float32)

    def spread(k):
        transform(k)
        send_core(k)

    cross(0)
    pl.semaphore_wait(barrier, len(peers))

    src_copies = {}
    for k in (2, 1, 3):
        copy = pltpu.make_async_remote_copy(
            src_ref=src_out.at[k - 1], dst_ref=src_in.at[k - 1],
            send_sem=src_s.at[k - 1], recv_sem=src_r.at[k - 1],
            device_id={"blk": (blk + k) % n_blk}, device_id_type=MESH,
        )
        copy.start()
        src_copies[k] = copy
    load_table.wait()
    spread(0)
    arrive(2)
    cross(2)
    spread(2)
    send_x(0)
    send_x(2)
    arrive(1)
    cross(1)
    spread(1)
    arrive(3)
    cross(3)
    spread(3)
    send_y(0)
    send_x(1)
    send_x(3)
    send_y(2)
    finish(0)
    send_y(1)
    finish(2)
    send_y(3)
    finish(1)
    finish(3)
    for copy in [*src_copies.values(), *core_copies.values(), *x_copies.values(), *y_copies.values()]:
        copy.wait_send()


def local(spectra, picks):
    freqs, width, chans = spectra.shape[1:]
    table = jnp.asarray(tables(width * lax.axis_size("tm")))
    dma = pltpu.SemaphoreType.DMA
    scratch = [
        pltpu.VMEM((2, F * W, C), jnp.bfloat16),
        pltpu.VMEM(table.shape, jnp.bfloat16),
        pltpu.VMEM((STEPS, 2 * SRC * NG, G * W), jnp.float32),
        pltpu.VMEM((STEPS - 1, 2 * SRC * NG, G * W), jnp.bfloat16),
        pltpu.VMEM((STEPS - 1, 2 * SRC * NG, G * W), jnp.bfloat16),
        pltpu.VMEM((STEPS, 2, 2, F, COLS), jnp.bfloat16),
        pltpu.VMEM((STEPS, 2, NX, NY * ROWS, COLS), jnp.float32),
        pltpu.VMEM((STEPS, NX, NY * ROWS, COLS), jnp.float32),
        pltpu.VMEM((STEPS, NX - 1, NY * ROWS, COLS), jnp.float32),
        pltpu.VMEM((STEPS, NY, ROWS, COLS), jnp.float32),
        pltpu.VMEM((STEPS, NY - 1, ROWS, COLS), jnp.float32),
        dma((2,)), dma((STEPS - 1,)), dma((STEPS - 1,)), dma((STEPS,)), dma((STEPS,)),
        dma((STEPS, NX - 1)), dma((STEPS, NX - 1)), dma((STEPS, NY - 1)), dma((STEPS, NY - 1)),
    ]
    any_space = pl.BlockSpec(memory_space=pl.ANY)
    operands = (spectra.reshape(2, freqs * width, chans), table, picks.T)
    got = pl.pallas_call(
        kernel,
        out_shape=jax.ShapeDtypeStruct((STEPS, SRC, ROWS, C), jnp.float32),
        in_specs=[any_space, any_space, pl.BlockSpec(memory_space=pltpu.SMEM)],
        out_specs=pl.BlockSpec(memory_space=pltpu.VMEM),
        scratch_shapes=scratch,
        compiler_params=pltpu.CompilerParams(
            collective_id=0, has_side_effects=True, vmem_limit_bytes=40 * 1024 * 1024
        ),
        name="correlate",
    )(*(pltpu.with_memory_space_constraint(value, pltpu.HBM) for value in operands))
    return jnp.transpose(got, (0, 2, 1, 3))


def solution(mesh):
    placed = (P(None, None, "tm", "blk"), P(None, "blk"))
    return jax.shard_map(
        local, mesh=mesh, in_specs=placed, out_specs=P(None, "tm", None, "blk"), check_vma=False
    )
```

```python
import functools
import math

import jax
import jax.numpy as jnp
import ml_dtypes
import numpy as np
from jax import lax
from jax.experimental import pallas as pl
from jax.experimental.pallas import tpu as pltpu
from jax.sharding import PartitionSpec as P

F = 512
LAGS = 512
W = 8
C = 128
STEPS = 4
SRC = 2
G = 32
NG = F // G
NX = 4
NY = 4
ROWS = 16
COLS = SRC * C
MESH = pl.DeviceIdType.MESH


def tables(windows):
    scale = 1.0 / math.sqrt(F * windows)
    core, x, ylo, i = np.meshgrid(np.arange(2), np.arange(NX), np.arange(2), np.arange(ROWS), indexing="ij")
    lag = (ylo * 128 + x * 32 + core * 16 + i).reshape(2, 1, 128, 1)
    freq = 2 * np.arange(F // 2)[None, :] + np.arange(2)[:, None]
    angle = 2.0 * np.pi / LAGS * (lag * freq.reshape(1, 2, 1, F // 2) % LAGS)
    full = (np.concatenate([np.cos(angle), -np.sin(angle)], axis=3) * scale).astype(np.float32)
    high = full.astype(ml_dtypes.bfloat16)
    low = (full - high.astype(np.float32)).astype(ml_dtypes.bfloat16)
    return np.stack([high, low], axis=1)


def kernel(
    spec_hbm, table_hbm, picks, out,
    spec, table, rows, src_out, src_in, x_ref, part, core_in, x_in, summed, y_in,
    load_sem, src_s, src_r, core_s, core_r, x_s, x_r, y_s, y_r,
):
    blk = lax.axis_index("blk")
    tm = lax.axis_index("tm")
    core = tm % 2
    xpos = (tm // 2) % NX
    ypos = tm // (2 * NX)
    n_blk = lax.axis_size("blk")

    def at(y, x, c):
        return {"tm": (y * NX + x) * 2 + c}

    load_spec = pltpu.make_async_copy(spec_hbm, spec, load_sem.at[0])
    load_table = pltpu.make_async_copy(table_hbm, table, load_sem.at[1])
    load_spec.start()
    load_table.start()

    barrier = pltpu.get_barrier_semaphore()
    peers = [at(ypos, xpos, 1 - core)]
    peers += [at(ypos, (xpos + d) % NX, core) for d in range(1, NX)]
    peers += [at((ypos + d) % NY, xpos, core) for d in range(1, NY)]
    for k in range(1, STEPS):
        peers += [{"blk": (blk + k) % n_blk}, {"blk": (blk + n_blk - k) % n_blk}]
    for peer in peers:
        pl.semaphore_signal(barrier, inc=1, device_id=peer, device_id_type=MESH)

    row_id = lax.broadcasted_iota(jnp.int32, (16, C), 0)
    lane_id = lax.broadcasted_iota(jnp.int32, (16, C), 1)
    chosen = jnp.full((16, C), -1, jnp.int32)
    for k in range(STEPS):
        for s in range(SRC):
            chosen = jnp.where(row_id == k * SRC + s, picks[s, k], chosen)
    one_hot = jnp.where(lane_id == chosen, 1.0, 0.0).astype(jnp.bfloat16)

    load_spec.wait()

    def select(g, carry):
        for p in range(2):
            got = lax.dot_general(
                one_hot, spec[p, pl.ds(pl.multiple_of(g * G * W, G * W), G * W), :],
                (((1,), (1,)), ((), ())), preferred_element_type=jnp.float32,
            )
            for k in range(STEPS):
                for s in range(SRC):
                    r = k * SRC + s
                    rows[k, pl.ds((p * SRC + s) * NG + g, 1), :] = got[r : r + 1, :]
        return carry

    lax.fori_loop(0, NG, select, 0, unroll=8)
    for k in range(1, STEPS):
        src_out[k - 1] = rows[k].astype(jnp.bfloat16)
    r_id = lax.broadcasted_iota(jnp.int32, (G, G * W), 0)
    l_id = lax.broadcasted_iota(jnp.int32, (G, G * W), 1)
    half = G // 2
    wanted = jnp.where(r_id < half, 2 * r_id, 2 * (r_id - half) + 1)
    mask = jnp.where(l_id // W == wanted, 1.0, 0.0)

    def cross(k):
        def body(g, carry):
            block = pl.ds(pl.multiple_of(g * G * W, G * W), G * W)
            both = jnp.concatenate([spec[0, block, :], spec[1, block, :]], axis=1)
            left = [
                (rows[k, pl.ds((p * SRC + s) * NG + g, 1), :] * mask).astype(jnp.bfloat16)
                for p in range(2)
                for s in range(SRC)
            ]
            term = jnp.dot(jnp.concatenate(left, axis=0), both, preferred_element_type=jnp.float32)
            count = SRC * G
            parts = (
                term[:count, :C] + term[count:, C:],
                term[:count, C:] - term[count:, :C],
            )
            for ri, total in enumerate(parts):
                high = total.astype(jnp.bfloat16)
                low = (total - high.astype(jnp.float32)).astype(jnp.bfloat16)
                for hl, value in enumerate((high, low)):
                    for s in range(SRC):
                        for eo in range(2):
                            top = s * G + eo * half
                            x_ref[
                                k, hl, eo,
                                pl.ds(pl.multiple_of(ri * (F // 2) + g * half, half), half),
                                s * C : (s + 1) * C,
                            ] = value[top : top + half]
            return carry

        lax.fori_loop(0, NG, body, 0, unroll=8)

    def transform(k):
        for h in range(2):
            both = []
            for eo in range(2):
                high = x_ref[k, 0, eo]
                low = x_ref[k, 1, eo]
                both.append(
                    jnp.dot(table[h, 0, eo], high, preferred_element_type=jnp.float32)
                    + jnp.dot(table[h, 0, eo], low, preferred_element_type=jnp.float32)
                    + jnp.dot(table[h, 1, eo], high, preferred_element_type=jnp.float32)
                )
            plus = both[0] + both[1]
            minus = both[0] - both[1]
            for x in range(NX):
                part[k, h, x, 0:32, :] = plus[x * 32 : x * 32 + 32]
                part[k, h, x, 32:64, :] = minus[x * 32 : x * 32 + 32]

    core_copies, x_copies, y_copies = {}, {}, {}

    def send_core(k):
        copy = pltpu.make_async_remote_copy(
            src_ref=part.at[k, 1 - core], dst_ref=core_in.at[k],
            send_sem=core_s.at[k], recv_sem=core_r.at[k],
            device_id=at(ypos, xpos, 1 - core), device_id_type=MESH,
        )
        copy.start()
        core_copies[k] = copy

    def send_x(k):
        core_copies[k].wait_recv()
        part[k, core] = part[k, core] + core_in[k]
        for d in (2, 1, 3):
            copy = pltpu.make_async_remote_copy(
                src_ref=part.at[k, core, (xpos + d) % NX], dst_ref=x_in.at[k, d - 1],
                send_sem=x_s.at[k, d - 1], recv_sem=x_r.at[k, d - 1],
                device_id=at(ypos, (xpos + d) % NX, core), device_id_type=MESH,
            )
            copy.start()
            x_copies[k, d] = copy

    def send_y(k):
        for d in range(1, NX):
            x_copies[k, d].wait_recv()
        total = part[k, core, xpos] + x_in[k, 0] + x_in[k, 1] + x_in[k, 2]
        for y in range(NY):
            summed[k, y] = total[y * ROWS : (y + 1) * ROWS]
        for d in range(1, NY):
            copy = pltpu.make_async_remote_copy(
                src_ref=summed.at[k, (ypos + d) % NY], dst_ref=y_in.at[k, d - 1],
                send_sem=y_s.at[k, d - 1], recv_sem=y_r.at[k, d - 1],
                device_id=at((ypos + d) % NY, xpos, core), device_id_type=MESH,
            )
            copy.start()
            y_copies[k, d] = copy

    def finish(k):
        for d in range(1, NY):
            y_copies[k, d].wait_recv()
        total = summed[k, ypos] + y_in[k, 0] + y_in[k, 1] + y_in[k, 2]
        for s in range(SRC):
            out[k, s] = total[:, s * C : (s + 1) * C]

    def arrive(k):
        src_copies[k].wait_recv()
        rows[k] = src_in[k - 1].astype(jnp.float32)

    def spread(k):
        transform(k)
        send_core(k)

    cross(0)
    pl.semaphore_wait(barrier, len(peers))

    src_copies = {}
    for k in (2, 1, 3):
        copy = pltpu.make_async_remote_copy(
            src_ref=src_out.at[k - 1], dst_ref=src_in.at[k - 1],
            send_sem=src_s.at[k - 1], recv_sem=src_r.at[k - 1],
            device_id={"blk": (blk + k) % n_blk}, device_id_type=MESH,
        )
        copy.start()
        src_copies[k] = copy
    load_table.wait()
    spread(0)
    send_x(0)
    arrive(2)
    cross(2)
    spread(2)
    send_x(2)
    arrive(1)
    cross(1)
    spread(1)
    send_x(1)
    arrive(3)
    cross(3)
    spread(3)
    send_y(0)
    send_y(2)
    send_x(3)
    finish(0)
    send_y(1)
    finish(2)
    send_y(3)
    finish(1)
    finish(3)
    for copy in [*src_copies.values(), *core_copies.values(), *x_copies.values(), *y_copies.values()]:
        copy.wait_send()


def local(spectra, picks):
    freqs, width, chans = spectra.shape[1:]
    table = jnp.asarray(tables(width * lax.axis_size("tm")))
    dma = pltpu.SemaphoreType.DMA
    scratch = [
        pltpu.VMEM((2, F * W, C), jnp.bfloat16),
        pltpu.VMEM(table.shape, jnp.bfloat16),
        pltpu.VMEM((STEPS, 2 * SRC * NG, G * W), jnp.float32),
        pltpu.VMEM((STEPS - 1, 2 * SRC * NG, G * W), jnp.bfloat16),
        pltpu.VMEM((STEPS - 1, 2 * SRC * NG, G * W), jnp.bfloat16),
        pltpu.VMEM((STEPS, 2, 2, F, COLS), jnp.bfloat16),
        pltpu.VMEM((STEPS, 2, NX, NY * ROWS, COLS), jnp.float32),
        pltpu.VMEM((STEPS, NX, NY * ROWS, COLS), jnp.float32),
        pltpu.VMEM((STEPS, NX - 1, NY * ROWS, COLS), jnp.float32),
        pltpu.VMEM((STEPS, NY, ROWS, COLS), jnp.float32),
        pltpu.VMEM((STEPS, NY - 1, ROWS, COLS), jnp.float32),
        dma((2,)), dma((STEPS - 1,)), dma((STEPS - 1,)), dma((STEPS,)), dma((STEPS,)),
        dma((STEPS, NX - 1)), dma((STEPS, NX - 1)), dma((STEPS, NY - 1)), dma((STEPS, NY - 1)),
    ]
    any_space = pl.BlockSpec(memory_space=pl.ANY)
    operands = (spectra.reshape(2, freqs * width, chans), table, picks.T)
    got = pl.pallas_call(
        kernel,
        out_shape=jax.ShapeDtypeStruct((STEPS, SRC, ROWS, C), jnp.float32),
        in_specs=[any_space, any_space, pl.BlockSpec(memory_space=pltpu.SMEM)],
        out_specs=pl.BlockSpec(memory_space=pltpu.VMEM),
        scratch_shapes=scratch,
        compiler_params=pltpu.CompilerParams(
            collective_id=0, has_side_effects=True, vmem_limit_bytes=40 * 1024 * 1024
        ),
        name="correlate",
    )(*(pltpu.with_memory_space_constraint(value, pltpu.HBM) for value in operands))
    return jnp.transpose(got, (0, 2, 1, 3))


def solution(mesh):
    placed = (P(None, None, "tm", "blk"), P(None, "blk"))
    return jax.shard_map(
        local, mesh=mesh, in_specs=placed, out_specs=P(None, "tm", None, "blk"), check_vma=False
    )
```

```python
import functools
import math

import jax
import jax.numpy as jnp
import ml_dtypes
import numpy as np
from jax import lax
from jax.experimental import pallas as pl
from jax.experimental.pallas import tpu as pltpu
from jax.sharding import PartitionSpec as P

F = 512
LAGS = 512
W = 8
C = 128
STEPS = 4
SRC = 2
G = 32
NG = F // G
NX = 4
NY = 4
ROWS = 16
COLS = SRC * C
MESH = pl.DeviceIdType.MESH


def tables(windows):
    scale = 1.0 / math.sqrt(F * windows)
    core, x, ylo, i = np.meshgrid(np.arange(2), np.arange(NX), np.arange(2), np.arange(ROWS), indexing="ij")
    lag = (ylo * 128 + x * 32 + core * 16 + i).reshape(2, 1, 128, 1)
    freq = 2 * np.arange(F // 2)[None, :] + np.arange(2)[:, None]
    angle = 2.0 * np.pi / LAGS * (lag * freq.reshape(1, 2, 1, F // 2) % LAGS)
    full = (np.concatenate([np.cos(angle), -np.sin(angle)], axis=3) * scale).astype(np.float32)
    high = full.astype(ml_dtypes.bfloat16)
    low = (full - high.astype(np.float32)).astype(ml_dtypes.bfloat16)
    return np.stack([high, low], axis=1)


def kernel(
    spec_hbm, table_hbm, picks, out,
    spec, table, rows, src_out, src_in, x_ref, part, core_in, x_in, summed, y_in,
    load_sem, src_s, src_r, core_s, core_r, x_s, x_r, y_s, y_r,
):
    blk = lax.axis_index("blk")
    tm = lax.axis_index("tm")
    core = tm % 2
    xpos = (tm // 2) % NX
    ypos = tm // (2 * NX)
    n_blk = lax.axis_size("blk")

    def at(y, x, c):
        return {"tm": (y * NX + x) * 2 + c}

    load_spec = pltpu.make_async_copy(spec_hbm, spec, load_sem.at[0])
    load_table = pltpu.make_async_copy(table_hbm, table, load_sem.at[1])
    load_spec.start()
    load_table.start()

    barrier = pltpu.get_barrier_semaphore()
    peers = [at(ypos, xpos, 1 - core)]
    peers += [at(ypos, (xpos + d) % NX, core) for d in range(1, NX)]
    peers += [at((ypos + d) % NY, xpos, core) for d in range(1, NY)]
    for k in range(1, STEPS):
        peers += [{"blk": (blk + k) % n_blk}, {"blk": (blk + n_blk - k) % n_blk}]
    for peer in peers:
        pl.semaphore_signal(barrier, inc=1, device_id=peer, device_id_type=MESH)

    row_id = lax.broadcasted_iota(jnp.int32, (16, C), 0)
    lane_id = lax.broadcasted_iota(jnp.int32, (16, C), 1)
    chosen = jnp.full((16, C), -1, jnp.int32)
    for k in range(STEPS):
        for s in range(SRC):
            chosen = jnp.where(row_id == k * SRC + s, picks[s, k], chosen)
    one_hot = jnp.where(lane_id == chosen, 1.0, 0.0).astype(jnp.bfloat16)

    load_spec.wait()

    def select(g, carry):
        for p in range(2):
            got = lax.dot_general(
                one_hot, spec[p, pl.ds(pl.multiple_of(g * G * W, G * W), G * W), :],
                (((1,), (1,)), ((), ())), preferred_element_type=jnp.float32,
            )
            for k in range(STEPS):
                for s in range(SRC):
                    r = k * SRC + s
                    rows[k, pl.ds((p * SRC + s) * NG + g, 1), :] = got[r : r + 1, :]
        return carry

    lax.fori_loop(0, NG, select, 0, unroll=16)
    for k in range(1, STEPS):
        src_out[k - 1] = rows[k].astype(jnp.bfloat16)
    r_id = lax.broadcasted_iota(jnp.int32, (G, G * W), 0)
    l_id = lax.broadcasted_iota(jnp.int32, (G, G * W), 1)
    half = G // 2
    wanted = jnp.where(r_id < half, 2 * r_id, 2 * (r_id - half) + 1)
    mask = jnp.where(l_id // W == wanted, 1.0, 0.0)

    def cross(k):
        def body(g, carry):
            block = pl.ds(pl.multiple_of(g * G * W, G * W), G * W)
            both = jnp.concatenate([spec[0, block, :], spec[1, block, :]], axis=1)
            left = [
                (rows[k, pl.ds((p * SRC + s) * NG + g, 1), :] * mask).astype(jnp.bfloat16)
                for p in range(2)
                for s in range(SRC)
            ]
            term = jnp.dot(jnp.concatenate(left, axis=0), both, preferred_element_type=jnp.float32)
            count = SRC * G
            parts = (
                term[:count, :C] + term[count:, C:],
                term[:count, C:] - term[count:, :C],
            )
            for ri, total in enumerate(parts):
                high = total.astype(jnp.bfloat16)
                low = (total - high.astype(jnp.float32)).astype(jnp.bfloat16)
                for hl, value in enumerate((high, low)):
                    for s in range(SRC):
                        for eo in range(2):
                            top = s * G + eo * half
                            x_ref[
                                k, hl, eo,
                                pl.ds(pl.multiple_of(ri * (F // 2) + g * half, half), half),
                                s * C : (s + 1) * C,
                            ] = value[top : top + half]
            return carry

        lax.fori_loop(0, NG, body, 0, unroll=16)

    def transform(k):
        for h in range(2):
            both = []
            for eo in range(2):
                high = x_ref[k, 0, eo]
                low = x_ref[k, 1, eo]
                both.append(
                    jnp.dot(table[h, 0, eo], high, preferred_element_type=jnp.float32)
                    + jnp.dot(table[h, 0, eo], low, preferred_element_type=jnp.float32)
                    + jnp.dot(table[h, 1, eo], high, preferred_element_type=jnp.float32)
                )
            plus = both[0] + both[1]
            minus = both[0] - both[1]
            for x in range(NX):
                part[k, h, x, 0:32, :] = plus[x * 32 : x * 32 + 32]
                part[k, h, x, 32:64, :] = minus[x * 32 : x * 32 + 32]

    core_copies, x_copies, y_copies = {}, {}, {}

    def send_core(k):
        copy = pltpu.make_async_remote_copy(
            src_ref=part.at[k, 1 - core], dst_ref=core_in.at[k],
            send_sem=core_s.at[k], recv_sem=core_r.at[k],
            device_id=at(ypos, xpos, 1 - core), device_id_type=MESH,
        )
        copy.start()
        core_copies[k] = copy

    def send_x(k):
        core_copies[k].wait_recv()
        part[k, core] = part[k, core] + core_in[k]
        for d in (2, 1, 3):
            copy = pltpu.make_async_remote_copy(
                src_ref=part.at[k, core, (xpos + d) % NX], dst_ref=x_in.at[k, d - 1],
                send_sem=x_s.at[k, d - 1], recv_sem=x_r.at[k, d - 1],
                device_id=at(ypos, (xpos + d) % NX, core), device_id_type=MESH,
            )
            copy.start()
            x_copies[k, d] = copy

    def send_y(k):
        for d in range(1, NX):
            x_copies[k, d].wait_recv()
        total = part[k, core, xpos] + x_in[k, 0] + x_in[k, 1] + x_in[k, 2]
        for y in range(NY):
            summed[k, y] = total[y * ROWS : (y + 1) * ROWS]
        for d in range(1, NY):
            copy = pltpu.make_async_remote_copy(
                src_ref=summed.at[k, (ypos + d) % NY], dst_ref=y_in.at[k, d - 1],
                send_sem=y_s.at[k, d - 1], recv_sem=y_r.at[k, d - 1],
                device_id=at((ypos + d) % NY, xpos, core), device_id_type=MESH,
            )
            copy.start()
            y_copies[k, d] = copy

    def finish(k):
        for d in range(1, NY):
            y_copies[k, d].wait_recv()
        total = summed[k, ypos] + y_in[k, 0] + y_in[k, 1] + y_in[k, 2]
        for s in range(SRC):
            out[k, s] = total[:, s * C : (s + 1) * C]

    def arrive(k):
        src_copies[k].wait_recv()
        rows[k] = src_in[k - 1].astype(jnp.float32)

    def spread(k):
        transform(k)
        send_core(k)

    cross(0)
    pl.semaphore_wait(barrier, len(peers))

    src_copies = {}
    for k in (2, 1, 3):
        copy = pltpu.make_async_remote_copy(
            src_ref=src_out.at[k - 1], dst_ref=src_in.at[k - 1],
            send_sem=src_s.at[k - 1], recv_sem=src_r.at[k - 1],
            device_id={"blk": (blk + k) % n_blk}, device_id_type=MESH,
        )
        copy.start()
        src_copies[k] = copy
    load_table.wait()
    spread(0)
    send_x(0)
    arrive(2)
    cross(2)
    spread(2)
    send_x(2)
    arrive(1)
    cross(1)
    spread(1)
    send_x(1)
    arrive(3)
    cross(3)
    spread(3)
    send_y(0)
    send_y(2)
    send_x(3)
    finish(0)
    send_y(1)
    finish(2)
    send_y(3)
    finish(1)
    finish(3)
    for copy in [*src_copies.values(), *core_copies.values(), *x_copies.values(), *y_copies.values()]:
        copy.wait_send()


def local(spectra, picks):
    freqs, width, chans = spectra.shape[1:]
    table = jnp.asarray(tables(width * lax.axis_size("tm")))
    dma = pltpu.SemaphoreType.DMA
    scratch = [
        pltpu.VMEM((2, F * W, C), jnp.bfloat16),
        pltpu.VMEM(table.shape, jnp.bfloat16),
        pltpu.VMEM((STEPS, 2 * SRC * NG, G * W), jnp.float32),
        pltpu.VMEM((STEPS - 1, 2 * SRC * NG, G * W), jnp.bfloat16),
        pltpu.VMEM((STEPS - 1, 2 * SRC * NG, G * W), jnp.bfloat16),
        pltpu.VMEM((STEPS, 2, 2, F, COLS), jnp.bfloat16),
        pltpu.VMEM((STEPS, 2, NX, NY * ROWS, COLS), jnp.float32),
        pltpu.VMEM((STEPS, NX, NY * ROWS, COLS), jnp.float32),
        pltpu.VMEM((STEPS, NX - 1, NY * ROWS, COLS), jnp.float32),
        pltpu.VMEM((STEPS, NY, ROWS, COLS), jnp.float32),
        pltpu.VMEM((STEPS, NY - 1, ROWS, COLS), jnp.float32),
        dma((2,)), dma((STEPS - 1,)), dma((STEPS - 1,)), dma((STEPS,)), dma((STEPS,)),
        dma((STEPS, NX - 1)), dma((STEPS, NX - 1)), dma((STEPS, NY - 1)), dma((STEPS, NY - 1)),
    ]
    any_space = pl.BlockSpec(memory_space=pl.ANY)
    operands = (spectra.reshape(2, freqs * width, chans), table, picks.T)
    got = pl.pallas_call(
        kernel,
        out_shape=jax.ShapeDtypeStruct((STEPS, SRC, ROWS, C), jnp.float32),
        in_specs=[any_space, any_space, pl.BlockSpec(memory_space=pltpu.SMEM)],
        out_specs=pl.BlockSpec(memory_space=pltpu.VMEM),
        scratch_shapes=scratch,
        compiler_params=pltpu.CompilerParams(
            collective_id=0, has_side_effects=True, vmem_limit_bytes=40 * 1024 * 1024
        ),
        name="correlate",
    )(*(pltpu.with_memory_space_constraint(value, pltpu.HBM) for value in operands))
    return jnp.transpose(got, (0, 2, 1, 3))


def solution(mesh):
    placed = (P(None, None, "tm", "blk"), P(None, "blk"))
    return jax.shard_map(
        local, mesh=mesh, in_specs=placed, out_specs=P(None, "tm", None, "blk"), check_vma=False
    )
```
